768 devices in a mesh: section: 64 (over y, z_hi, x), dp: 12 (over z_lo, core).
Axes of the slice: x: 4, y: 8, z: 12 (z_hi: 2, z_lo: 6; z = z_hi * 6 + z_lo), core: 2. Of those that a mesh axis runs over, the one named last changes fastest.
Arguments:
- stash_q: bfloat16 [64, 12, 128, 4096], P('section', 'dp'), may hold values from -5.5 to 5.5
- stash_kv: bfloat16 [64, 12, 128, 1024], P('section', 'dp'), may hold values from -5.5 to 5.5
- upstream: bfloat16 [64, 12, 128, 4096], P('section', 'dp'), may hold values from -6 to 6
- lengths: int32 [12], P('dp'), may hold values from 2 to 128, as said below
- domains: int32 [12], P('dp'), may hold values from 0 to 6
- domain_weight: float32 [7], replicated, may hold values from 0.3 to 3
Outputs:
- grad_q: bfloat16 [64, 12, 128, 4096], P('section', 'dp')
- grad_kv: bfloat16 [64, 12, 128, 1024], P('section', 'dp')
The draws below stay inside these ranges and needn't reach their ends.
Inputs may be any that keep to these rules, and one draw needn't show every extreme that they name: `lengths`: some micro-batch has exactly 128 live tokens.
All inputs are finite; a program needn't handle non-finite values.
Results may differ from the reference program's by a relative error of at most 0.006.
Values may be sent and summed in bfloat16 or wider, within the bound.
No kernel may reach another device: no remote copies, remote signals or barrier semaphores. Data moves between devices by JAX's collectives and lax.ppermute only.
A program may use at most 32 MiB of HBM per device.

```python
import math
import jax
import jax.numpy as jnp
from jax import lax

QUERY_HEADS = 32
KEY_VALUE_HEADS = 4
HEAD_SIZE = 128
DOMAINS = 7
SEQUENCE_TOKENS = 128
MB = 1
RELAY_SECTIONS = 64
MICRO_BATCHES = 12


def draw_stash_q(key, part):
    baseline_loss = jnp.clip(jax.random.normal(jax.random.fold_in(key, 1), (RELAY_SECTIONS, MICRO_BATCHES, SEQUENCE_TOKENS, QUERY_HEADS * HEAD_SIZE), jnp.float32), -4.0, 4.0)
    return baseline_loss.astype(jnp.bfloat16)


def draw_stash_kv(key, part):
    baseline_loss = jnp.clip(jax.random.normal(jax.random.fold_in(key, 2), (RELAY_SECTIONS, MICRO_BATCHES, SEQUENCE_TOKENS, 2 * KEY_VALUE_HEADS * HEAD_SIZE), jnp.float32), -4.0, 4.0)
    return baseline_loss.astype(jnp.bfloat16)


def draw_lengths(key, part):
    replicas = MICRO_BATCHES // MB
    replica = jnp.arange(MICRO_BATCHES, dtype=jnp.int32) // MB
    lower = 2 + (SEQUENCE_TOKENS * 3 // 4 - 2) * replica // max(replicas - 1, 1)
    upper = lower + SEQUENCE_TOKENS // 4 + 1
    upper = jnp.minimum(upper, SEQUENCE_TOKENS + 1)
    drawn = jax.random.randint(jax.random.fold_in(key, 3), (MICRO_BATCHES,), lower, upper).astype(jnp.int32)
    index = jnp.arange(MICRO_BATCHES, dtype=jnp.int32)
    drawn = jnp.where(index == MICRO_BATCHES - 1, SEQUENCE_TOKENS, drawn)
    drawn = jnp.where(index == 0, 2, drawn)
    return drawn.astype(jnp.int32)


def touch_ends(result, stream_key, smallest, high):
    spot = [jax.random.randint(jax.random.fold_in(stream_key, axis), (), 0, length) for axis, length in enumerate(result.shape)]
    longest = result.shape.index(max(result.shape))
    neighbour = spot[:longest] + [(spot[longest] + 1) % result.shape[longest]] + spot[longest + 1:]
    return result.at[tuple(spot)].set(smallest).at[tuple(neighbour)].set(high)


def level_of(own_key, extent, pieces, least, high):
    factor_of, own = 1.0, jax.random.fold_in(own_key, 6)
    for dim, parts in pieces:
        draws = jnp.exp(jax.random.uniform(jax.random.fold_in(own, dim), (parts,), jnp.float32, least / len(pieces), high / len(pieces)))
        factor_of = factor_of * jnp.repeat(draws, extent[dim] // parts).reshape([-1 if axis == dim else 1 for axis in range(len(extent))])
    return factor_of


def centred(stream_key, extent, width, limit, pieces=(), held_as=jnp.bfloat16):
    values = jax.random.normal(stream_key, extent, jnp.float32) * width
    if len(pieces) > 0:
        values = level_of(stream_key, extent, pieces, -0.22, 0.18) * values
    return jnp.clip(values, min=-limit, max=limit).astype(held_as)


def setup_inputs(seed: int = 0) -> dict:
    seeds = jax.random.split(jax.random.key(seed), 7)
    return {
        "stash_q": draw_stash_q(jax.random.fold_in(seeds[6], 71), 0),
        "stash_kv": draw_stash_kv(jax.random.fold_in(seeds[6], 71), 0),
        "upstream": centred(seeds[2], (RELAY_SECTIONS, MICRO_BATCHES, SEQUENCE_TOKENS, QUERY_HEADS * HEAD_SIZE), 1.0, 6.0, ((0, 64), (1, 12))),
        "lengths": draw_lengths(jax.random.fold_in(seeds[6], 71), 0),
        "domains": touch_ends(jax.random.randint(seeds[4], (MICRO_BATCHES,), 0, DOMAINS), jax.random.fold_in(seeds[4], 1), 0, DOMAINS - 1).astype(jnp.int32),
        "domain_weight": jnp.clip(jnp.exp(jax.random.uniform(seeds[5], (DOMAINS,), jnp.float32, math.log(0.3), math.log(3.0))), 0.3, 3.0),
    }


def backward_block(query_rows, paired_stash, grads, lengths, factor):
    batch_list = query_rows.shape[0]
    group_count = QUERY_HEADS // KEY_VALUE_HEADS
    inv_root = 1.0 / math.sqrt(HEAD_SIZE)
    query_head_rows = query_rows.astype(jnp.float32).reshape(batch_list, SEQUENCE_TOKENS, KEY_VALUE_HEADS, group_count, HEAD_SIZE)
    key_head_rows = paired_stash[..., :KEY_VALUE_HEADS * HEAD_SIZE].astype(jnp.float32).reshape(batch_list, SEQUENCE_TOKENS, KEY_VALUE_HEADS, HEAD_SIZE)
    value_head_rows = paired_stash[..., KEY_VALUE_HEADS * HEAD_SIZE:].astype(jnp.float32).reshape(batch_list, SEQUENCE_TOKENS, KEY_VALUE_HEADS, HEAD_SIZE)
    row_index = jnp.arange(SEQUENCE_TOKENS, dtype=jnp.int32)[:, None]
    col_index = jnp.arange(SEQUENCE_TOKENS, dtype=jnp.int32)[None, :]
    allowed = (col_index <= row_index)[None] & (col_index[None] < lengths[:, None, None])
    live = jnp.arange(SEQUENCE_TOKENS, dtype=jnp.int32)[None, :] < lengths[:, None]
    gradient_heads = jnp.where(live[:, :, None], grads, jnp.zeros((), grads.dtype))
    gradient_heads = gradient_heads.astype(jnp.float32).reshape(batch_list, SEQUENCE_TOKENS, KEY_VALUE_HEADS, group_count, HEAD_SIZE)
    scores = jnp.einsum('bikgd,bjkd->bkgij', query_head_rows, key_head_rows) * inv_root
    scores = jnp.where(allowed[:, None, None], scores, jnp.float32(-1e+30))
    peak = lax.optimization_barrier(jnp.max(scores, axis=-1, keepdims=True))
    expo = jnp.exp(scores - peak)
    probability = expo / lax.optimization_barrier(jnp.sum(expo, axis=-1, keepdims=True))
    prob_half = probability.astype(jnp.bfloat16).astype(jnp.float32)
    value_gradient = jnp.einsum('bkgij,bikgd->bjkd', prob_half, gradient_heads)
    prob_grad = jnp.einsum('bikgd,bjkd->bkgij', gradient_heads, value_head_rows)
    row_total = lax.optimization_barrier(jnp.sum(probability * prob_grad, axis=-1, keepdims=True))
    score_grad = (probability * (prob_grad - row_total) * inv_root).astype(jnp.bfloat16).astype(jnp.float32)
    query_grad = jnp.einsum('bkgij,bjkd->bikgd', score_grad, key_head_rows)
    key_gradient = jnp.einsum('bkgij,bikgd->bjkd', score_grad, query_head_rows)
    row_scales = factor[:, None, None]
    out_q = (query_grad.reshape(batch_list, SEQUENCE_TOKENS, QUERY_HEADS * HEAD_SIZE) * row_scales).astype(jnp.bfloat16)
    output_key = key_gradient.reshape(batch_list, SEQUENCE_TOKENS, KEY_VALUE_HEADS * HEAD_SIZE) * row_scales
    output_value = value_gradient.reshape(batch_list, SEQUENCE_TOKENS, KEY_VALUE_HEADS * HEAD_SIZE) * row_scales
    return (out_q, jnp.concatenate([output_key, output_value], axis=-1).astype(jnp.bfloat16))

def reference(stash_q, stash_kv, upstream, lengths, domains, domain_weight):
    domain_ids = jnp.arange(DOMAINS, dtype=jnp.int32)
    onehot = domains[:, None] == domain_ids[None, :]
    counts = lax.optimization_barrier(jnp.sum(jnp.where(onehot, lengths[:, None], 0), axis=0)).astype(jnp.int32)
    count_float = counts.astype(jnp.float32)
    token_total = jnp.sum(count_float)
    own_count = lax.optimization_barrier(jnp.sum(jnp.where(onehot, count_float[None, :], jnp.float32(0.0)), axis=1))
    weight = lax.optimization_barrier(jnp.sum(jnp.where(onehot, domain_weight[None, :], jnp.float32(0.0)), axis=1))
    factor = weight * token_total / (DOMAINS * own_count)
    partner_q = jnp.roll(stash_q, RELAY_SECTIONS // 2, axis=0)
    partner_kv = jnp.roll(stash_kv, RELAY_SECTIONS // 2, axis=0)
    next_grads = jnp.roll(upstream, -1, axis=0)

    def one_section(items):
        return backward_block(items[0], items[1], items[2], lengths, factor)
    grad_q, grad_kv = lax.map(one_section, (partner_q, partner_kv, next_grads))
    return (grad_q, grad_kv)
```

```python
import functools
import math

import jax
import jax.numpy as jnp
from jax import lax
from jax.experimental import pallas as pl
from jax.experimental.pallas import tpu as pltpu
from jax.sharding import PartitionSpec as P

KV_HEADS = 4
GROUP = 8
HEAD = 128
DOMAINS = 7
TOKENS = 128
REPLICAS = 12
NY, NZ, NX = 8, 2, 4

INV_ROOT = 1.0 / math.sqrt(HEAD)
LOG_SCALE = INV_ROOT * math.log2(math.e)
NT = (((1,), (1,)), ((), ()))
TN = (((0,), (0,)), ((), ()))


def section_pairs(move):
    pairs = []
    for y in range(NY):
        for z in range(NZ):
            for x in range(NX):
                to = move(y, z, x)
                if to is not None:
                    ty, tz, tx = to
                    pairs.append(((y * NZ + z) * NX + x, ((ty % NY) * NZ + tz % NZ) * NX + tx % NX))
    return pairs


def moved(array, move):
    return lax.ppermute(array, "section", section_pairs(move))


def opposite(y, z, x):
    return y + 4, z, x


def previous(y, z, x):
    return (y, z, x - 1) if x else (y - 1 + z, z + 1, 3)


def x_ring(y, z, x):
    return y, z, x - 1


def facts_of(facts_ref):
    number = lambda value: value.astype(jnp.int32)
    own = number(facts_ref[0, 3])
    domain = facts_ref[own, 1]
    total = jnp.float32(0)
    count = jnp.float32(0)
    for b in range(REPLICAS):
        n = facts_ref[b, 0]
        total += n
        count += jnp.where(facts_ref[b, 1] == domain, n, jnp.float32(0))
    weight = jnp.full((1, HEAD), facts_ref[0, 4 + number(domain)], jnp.float32)
    total = jnp.full((1, HEAD), total, jnp.float32)
    count = jnp.full((1, HEAD), count, jnp.float32)
    return number(facts_ref[own, 0]), number(facts_ref[0, 2]) == NX - 1, weight * total / (DOMAINS * count)


def one_group(live_tokens, factor, query, key, value, grad):
    width = GROUP * TOKENS
    j = lax.broadcasted_iota(jnp.int32, (TOKENS, width), 0)
    i = lax.broadcasted_iota(jnp.int32, (TOKENS, width), 1) % TOKENS
    allowed = (j <= i) & (j < live_tokens)
    live = (lax.broadcasted_iota(jnp.int32, (1, width), 1) % TOKENS) < live_tokens
    scores = lax.dot_general(key, query, NT, preferred_element_type=jnp.float32)
    prob_grad = lax.dot_general(value, grad, NT, preferred_element_type=jnp.float32)
    scores = jnp.where(allowed, scores, jnp.float32(-1e30))
    peak = jnp.max(scores, axis=0, keepdims=True)
    expo = jnp.exp2((scores - peak) * LOG_SCALE)
    share = jnp.where(live, 1.0 / jnp.sum(expo, axis=0, keepdims=True), 0.0)
    prob = expo * share
    value_grad = jnp.dot(prob.astype(jnp.bfloat16), grad, preferred_element_type=jnp.float32)
    row_total = jnp.sum(prob * prob_grad, axis=0, keepdims=True)
    score_grad = (prob * (prob_grad - row_total) * INV_ROOT).astype(jnp.bfloat16)
    key_grad = jnp.dot(score_grad, query, preferred_element_type=jnp.float32)
    query_grad = lax.dot_general(score_grad, key, TN, preferred_element_type=jnp.float32)
    return (
        (query_grad * factor).astype(jnp.bfloat16),
        (key_grad * factor).astype(jnp.bfloat16),
        (value_grad * factor).astype(jnp.bfloat16),
    )


def kernel(groups, parts, *refs):
    facts_ref, q_ref, kv_ref = refs[:3]
    grads = refs[3:-5]
    out_q, out_kv, dq, dkv, sem = refs[-5:]
    live_tokens, far, factor = facts_of(facts_ref)
    copies = []
    for at, group in enumerate(groups):
        queries, gradients = [], []
        for head in range(at * GROUP, (at + 1) * GROUP):
            queries.append(q_ref[:, head * HEAD : (head + 1) * HEAD])
            plain, other, column, other_column = parts[head]
            g = grads[plain][:, column : column + HEAD]
            if other is not None:
                g = jnp.where(far, grads[other][:, other_column : other_column + HEAD], g)
            gradients.append(g)
        key = kv_ref[:, group * HEAD : (group + 1) * HEAD]
        value = kv_ref[:, (KV_HEADS + group) * HEAD : (KV_HEADS + group + 1) * HEAD]
        query_grad, key_grad, value_grad = one_group(
            live_tokens, factor, jnp.concatenate(queries, 0), key, value, jnp.concatenate(gradients, 0)
        )
        for t in range(GROUP):
            dq[at, :, t * HEAD : (t + 1) * HEAD] = query_grad[t * TOKENS : (t + 1) * TOKENS]
        dkv[2 * at] = key_grad
        dkv[2 * at + 1] = value_grad
        span = GROUP * HEAD
        for n, (src, dst) in enumerate(
            (
                (dq.at[at], out_q.at[:, group * span : (group + 1) * span]),
                (dkv.at[2 * at], out_kv.at[:, group * HEAD : (group + 1) * HEAD]),
                (dkv.at[2 * at + 1], out_kv.at[:, (KV_HEADS + group) * HEAD : (KV_HEADS + group + 1) * HEAD]),
            )
        ):
            copy = pltpu.make_async_copy(src, dst, sem.at[3 * at + n])
            copy.start()
            copies.append(copy)
    for copy in copies:
        copy.wait()


def attend(groups, parts, facts, arrays, outputs=()):
    vmem = pl.BlockSpec(memory_space=pltpu.VMEM)
    smem = pl.BlockSpec(memory_space=pltpu.SMEM)
    hbm = pl.BlockSpec(memory_space=pl.ANY)
    count = len(groups)
    operands = (facts, *arrays, *outputs)
    first = 1 + len(arrays)
    elements = count * GROUP * TOKENS * HEAD
    return pl.pallas_call(
        functools.partial(kernel, groups, parts),
        out_shape=(
            jax.ShapeDtypeStruct((TOKENS, KV_HEADS * GROUP * HEAD), jnp.bfloat16),
            jax.ShapeDtypeStruct((TOKENS, 2 * KV_HEADS * HEAD), jnp.bfloat16),
        ),
        in_specs=[smem] + [vmem] * len(arrays) + [hbm] * len(outputs),
        out_specs=(hbm, hbm),
        scratch_shapes=[
            pltpu.VMEM((count, TOKENS, GROUP * HEAD), jnp.bfloat16),
            pltpu.VMEM((2 * count, TOKENS, HEAD), jnp.bfloat16),
            pltpu.SemaphoreType.DMA((3 * count,)),
        ],
        input_output_aliases={first + i: i for i in range(len(outputs))},
        compiler_params=pltpu.CompilerParams(vmem_limit_bytes=24 << 20),
        cost_estimate=pl.CostEstimate(flops=10 * elements * TOKENS, bytes_accessed=6 * elements, transcendentals=elements),
    )(*operands)


def across(column):
    return lambda y, z, x: (y - 1 + z, z + 1, 3) if x == column else None


def body(stash_q, stash_kv, upstream, lengths, domains, domain_weight):
    x = lax.axis_index("section") % NX
    span = GROUP * HEAD
    kv = moved(stash_kv, opposite)
    q_most = moved(stash_q[..., : 3 * span], opposite)
    q_last = moved(stash_q[..., 3 * span :], opposite)
    part = lambda first, count: upstream[..., first * span : (first + count) * span]
    b_near = moved(part(1, 1), x_ring)
    c_mid = moved(part(2, 1), lambda y, z, x: (y, z, 1) if x == 0 else None)
    d_mid = moved(part(3, 1), lambda y, z, x: (y, z, 2) if x == 0 else None)
    cd_near = moved(part(2, 2), lambda y, z, x: (y, z, x - 1) if x else None)
    a_all = moved(part(0, 1), previous)
    b_far = moved(b_near, across(3))
    c_far = moved(c_mid, across(1))
    d_far = moved(d_mid, across(2))
    own = jnp.concatenate([lengths, domains, x[None]]).astype(jnp.float32)
    to = jnp.arange(REPLICAS, dtype=jnp.float32)[:, None]
    row = lambda v: jnp.broadcast_to(v[None], (REPLICAS, v.shape[0]))
    facts = jnp.concatenate([row(own), to, row(domain_weight)], axis=1)
    facts = lax.all_to_all(facts, "dp", 0, 0, tiled=True)
    flat = lambda a: a.reshape(a.shape[2:])
    column = lambda h: (h % GROUP) * HEAD
    parts = [(0, None, column(h), 0) for h in range(8)]
    parts += [(1, 3, column(h), column(h)) for h in range(8)]
    parts += [(2, 4, column(h), column(h)) for h in range(8)]
    last = [(0, 1, column(h) + span, column(h)) for h in range(8)]
    arrays = (q_most, kv, a_all, b_near, cd_near, b_far, c_far)
    outs = attend((0, 1, 2), parts, facts, [flat(a) for a in arrays])
    arrays = (q_last, kv, cd_near, d_far)
    out_q, out_kv = attend((3,), last, facts, [flat(a) for a in arrays], outs)
    return out_q[None, None], out_kv[None, None]


def solution(mesh):
    spec = P("section", "dp", None, None)
    return jax.shard_map(
        body,
        mesh=mesh,
        in_specs=(spec, spec, spec, P("dp"), P("dp"), P()),
        out_specs=(spec, spec),
        check_vma=False,
    )
```

```python
import functools
import math

import jax
import jax.numpy as jnp
from jax import lax
from jax.experimental import pallas as pl
from jax.experimental.pallas import tpu as pltpu
from jax.sharding import PartitionSpec as P

KV_HEADS = 4
GROUP = 8
HEAD = 128
DOMAINS = 7
TOKENS = 128
REPLICAS = 12
NY, NZ, NX = 8, 2, 4

INV_ROOT = 1.0 / math.sqrt(HEAD)
LOG_SCALE = INV_ROOT * math.log2(math.e)
NT = (((1,), (1,)), ((), ()))
TN = (((0,), (0,)), ((), ()))


def section_pairs(move):
    pairs = []
    for y in range(NY):
        for z in range(NZ):
            for x in range(NX):
                to = move(y, z, x)
                if to is not None:
                    ty, tz, tx = to
                    pairs.append(((y * NZ + z) * NX + x, ((ty % NY) * NZ + tz % NZ) * NX + tx % NX))
    return pairs


def moved(array, move):
    return lax.ppermute(array, "section", section_pairs(move))


def opposite(y, z, x):
    return y + 4, z, x


def previous(y, z, x):
    return (y, z, x - 1) if x else (y - 1 + z, z + 1, 3)


def x_ring(y, z, x):
    return y, z, x - 1


def facts_of(facts_ref):
    facts = facts_ref[...]
    row = lax.broadcasted_iota(jnp.int32, (REPLICAS, 1), 0).astype(jnp.float32)
    own = jnp.sum(jnp.where(row == facts[:, 3:4], facts, 0.0), axis=0, keepdims=True)
    lengths, domains = facts[:, 0:1], facts[:, 1:2]
    domain = own[:, 1:2]
    total = jnp.sum(lengths, axis=0, keepdims=True)
    count = jnp.sum(jnp.where(domains == domain, lengths, 0.0), axis=0, keepdims=True)
    ids = lax.broadcasted_iota(jnp.int32, (1, DOMAINS), 1).astype(jnp.float32)
    weight = jnp.sum(jnp.where(ids == domain, own[:, 4 : 4 + DOMAINS], 0.0), axis=1, keepdims=True)
    return own[:, 0:1].astype(jnp.int32), own[:, 2:3] == NX - 1, weight * total / (DOMAINS * count)


def one_group(live_tokens, factor, query, key, value, grad):
    width = GROUP * TOKENS
    j = lax.broadcasted_iota(jnp.int32, (TOKENS, width), 0)
    i = lax.broadcasted_iota(jnp.int32, (TOKENS, width), 1) % TOKENS
    allowed = (j <= i) & (j < live_tokens)
    live = (lax.broadcasted_iota(jnp.int32, (1, width), 1) % TOKENS) < live_tokens
    scores = lax.dot_general(key, query, NT, preferred_element_type=jnp.float32)
    prob_grad = lax.dot_general(value, grad, NT, preferred_element_type=jnp.float32)
    scores = jnp.where(allowed, scores, jnp.float32(-1e30))
    peak = jnp.max(scores, axis=0, keepdims=True)
    expo = jnp.exp2((scores - peak) * LOG_SCALE)
    share = jnp.where(live, 1.0 / jnp.sum(expo, axis=0, keepdims=True), 0.0)
    prob = expo * share
    value_grad = jnp.dot(prob.astype(jnp.bfloat16), grad, preferred_element_type=jnp.float32)
    row_total = jnp.sum(prob * prob_grad, axis=0, keepdims=True)
    score_grad = (prob * (prob_grad - row_total) * INV_ROOT).astype(jnp.bfloat16)
    key_grad = jnp.dot(score_grad, query, preferred_element_type=jnp.float32)
    query_grad = lax.dot_general(score_grad, key, TN, preferred_element_type=jnp.float32)
    return (
        (query_grad * factor).astype(jnp.bfloat16),
        (key_grad * factor).astype(jnp.bfloat16),
        (value_grad * factor).astype(jnp.bfloat16),
    )


def kernel(groups, parts, *refs):
    facts_ref, kv_ref, q_ref = refs[:3]
    out_q, out_kv, dq, dkv, sem = refs[-5:]
    grads = refs[3:-5]
    live_tokens, far, factor = facts_of(facts_ref)
    copies = []
    for at, group in enumerate(groups):
        queries, gradients = [], []
        for head in range(at * GROUP, (at + 1) * GROUP):
            queries.append(q_ref[:, head * HEAD : (head + 1) * HEAD])
            plain, other, column, other_column = parts[head]
            g = grads[plain][:, column : column + HEAD]
            if other is not None:
                g = jnp.where(far, grads[other][:, other_column : other_column + HEAD], g)
            gradients.append(g)
        key = kv_ref[:, group * HEAD : (group + 1) * HEAD]
        value = kv_ref[:, (KV_HEADS + group) * HEAD : (KV_HEADS + group + 1) * HEAD]
        query_grad, key_grad, value_grad = one_group(
            live_tokens, factor, jnp.concatenate(queries, 0), key, value, jnp.concatenate(gradients, 0)
        )
        for t in range(GROUP):
            dq[at, :, t * HEAD : (t + 1) * HEAD] = query_grad[t * TOKENS : (t + 1) * TOKENS]
        dkv[2 * at] = key_grad
        dkv[2 * at + 1] = value_grad
        span = GROUP * HEAD
        for n, (src, dst) in enumerate(
            (
                (dq.at[at], out_q.at[:, group * span : (group + 1) * span]),
                (dkv.at[2 * at], out_kv.at[:, group * HEAD : (group + 1) * HEAD]),
                (dkv.at[2 * at + 1], out_kv.at[:, (KV_HEADS + group) * HEAD : (KV_HEADS + group + 1) * HEAD]),
            )
        ):
            copy = pltpu.make_async_copy(src, dst, sem.at[3 * at + n])
            copy.start()
            copies.append(copy)
    for copy in copies:
        copy.wait()


def attend(groups, parts, facts, arrays, outputs=()):
    vmem = pl.BlockSpec(memory_space=pltpu.VMEM)
    hbm = pl.BlockSpec(memory_space=pl.ANY)
    count = len(groups)
    operands = (facts, *arrays, *outputs)
    first = 1 + len(arrays)
    elements = count * GROUP * TOKENS * HEAD
    return pl.pallas_call(
        functools.partial(kernel, groups, parts),
        out_shape=(
            jax.ShapeDtypeStruct((TOKENS, KV_HEADS * GROUP * HEAD), jnp.bfloat16),
            jax.ShapeDtypeStruct((TOKENS, 2 * KV_HEADS * HEAD), jnp.bfloat16),
        ),
        in_specs=[vmem] * first + [hbm] * len(outputs),
        out_specs=(hbm, hbm),
        scratch_shapes=[
            pltpu.VMEM((count, TOKENS, GROUP * HEAD), jnp.bfloat16),
            pltpu.VMEM((2 * count, TOKENS, HEAD), jnp.bfloat16),
            pltpu.SemaphoreType.DMA((3 * count,)),
        ],
        input_output_aliases={first + i: i for i in range(len(outputs))},
        compiler_params=pltpu.CompilerParams(vmem_limit_bytes=24 << 20),
        cost_estimate=pl.CostEstimate(flops=10 * elements * TOKENS, bytes_accessed=6 * elements, transcendentals=elements),
    )(*operands)


def across(column):
    return lambda y, z, x: (y - 1 + z, z + 1, 3) if x == column else None


def body(stash_q, stash_kv, upstream, lengths, domains, domain_weight):
    x = lax.axis_index("section") % NX
    span = GROUP * HEAD
    kv = moved(stash_kv, opposite)
    q_most = moved(stash_q[..., : 3 * span], opposite)
    q_last = moved(stash_q[..., 3 * span :], opposite)
    part = lambda first, count: upstream[..., first * span : (first + count) * span]
    b_near = moved(part(1, 1), x_ring)
    c_mid = moved(part(2, 1), lambda y, z, x: (y, z, 1) if x == 0 else None)
    d_mid = moved(part(3, 1), lambda y, z, x: (y, z, 2) if x == 0 else None)
    cd_near = moved(part(2, 2), lambda y, z, x: (y, z, x - 1) if x else None)
    a_all = moved(part(0, 1), previous)
    b_far = moved(b_near, across(3))
    c_far = moved(c_mid, across(1))
    d_far = moved(d_mid, across(2))
    own = jnp.concatenate([lengths, domains, x[None]]).astype(jnp.float32)
    to = jnp.arange(REPLICAS, dtype=jnp.float32)[:, None]
    row = lambda v: jnp.broadcast_to(v[None], (REPLICAS, v.shape[0]))
    facts = jnp.concatenate([row(own), to, row(domain_weight)], axis=1)
    facts = lax.all_to_all(facts, "dp", 0, 0, tiled=True)
    flat = lambda a: a.reshape(a.shape[2:])
    column = lambda h: (h % GROUP) * HEAD
    parts = [(0, None, column(h), 0) for h in range(8)]
    parts += [(1, 3, column(h), column(h)) for h in range(8)]
    parts += [(2, 4, column(h), column(h)) for h in range(8)]
    last = [(0, 1, column(h) + span, column(h)) for h in range(8)]
    arrays = (kv, q_most, a_all, b_near, cd_near, b_far, c_far)
    outs = attend((0, 1, 2), parts, facts, [flat(a) for a in arrays])
    arrays = (kv, q_last, cd_near, d_far)
    out_q, out_kv = attend((3,), last, facts, [flat(a) for a in arrays], outs)
    return out_q[None, None], out_kv[None, None]


def solution(mesh):
    spec = P("section", "dp", None, None)
    return jax.shard_map(
        body,
        mesh=mesh,
        in_specs=(spec, spec, spec, P("dp"), P("dp"), P()),
        out_specs=(spec, spec),
        check_vma=False,
    )
```

```python
import functools
import math

import jax
import jax.numpy as jnp
from jax import lax
from jax.experimental import pallas as pl
from jax.experimental.pallas import tpu as pltpu
from jax.sharding import PartitionSpec as P

KV_HEADS = 4
GROUP = 8
HEAD = 128
DOMAINS = 7
TOKENS = 128
REPLICAS = 12
NY, NZ, NX = 8, 2, 4

INV_ROOT = 1.0 / math.sqrt(HEAD)
LOG_SCALE = INV_ROOT * math.log2(math.e)
NT = (((1,), (1,)), ((), ()))
TN = (((0,), (0,)), ((), ()))


def section_pairs(move):
    pairs = []
    for y in range(NY):
        for z in range(NZ):
            for x in range(NX):
                to = move(y, z, x)
                if to is not None:
                    ty, tz, tx = to
                    pairs.append(((y * NZ + z) * NX + x, ((ty % NY) * NZ + tz % NZ) * NX + tx % NX))
    return pairs


def device_pairs(move):
    pairs = []
    for y in range(NY):
        for z in range(NZ):
            for x in range(NX):
                for r in range(REPLICAS):
                    to = move(y, z, r)
                    if to is not None:
                        ty, tr = to
                        section = lambda v: ((v % NY) * NZ + z) * NX + x
                        pairs.append((section(y) * REPLICAS + r, section(ty) * REPLICAS + tr))
    return pairs


def moved_each(array, move):
    return lax.ppermute(array, ("section", "dp"), device_pairs(move))


def turned(y, z, replica):
    return (z == 1) & (replica % 2 == 0) & (y % 4 == 1)


def moved(array, move):
    return lax.ppermute(array, "section", section_pairs(move))


def opposite(y, z, x):
    return y + 4, z, x


def facts_of(facts_ref):
    facts = facts_ref[...]
    row = lax.broadcasted_iota(jnp.int32, (REPLICAS, 1), 0).astype(jnp.float32)
    own = jnp.sum(jnp.where(row == facts[:, 4:5], facts, 0.0), axis=0, keepdims=True)
    lengths, domains = facts[:, 0:1], facts[:, 1:2]
    domain = own[:, 1:2]
    total = jnp.sum(lengths, axis=0, keepdims=True)
    count = jnp.sum(jnp.where(domains == domain, lengths, 0.0), axis=0, keepdims=True)
    ids = lax.broadcasted_iota(jnp.int32, (1, DOMAINS), 1).astype(jnp.float32)
    weight = jnp.sum(jnp.where(ids == domain, own[:, 5 : 5 + DOMAINS], 0.0), axis=1, keepdims=True)
    return own[:, 0:1].astype(jnp.int32), own[:, 2:3] > 0.5, own[:, 3:4] > 0.5, weight * total / (DOMAINS * count)


def one_group(live_tokens, factor, query, key, value, grad):
    width = GROUP * TOKENS
    j = lax.broadcasted_iota(jnp.int32, (TOKENS, width), 0)
    i = lax.broadcasted_iota(jnp.int32, (TOKENS, width), 1) % TOKENS
    allowed = (j <= i) & (j < live_tokens)
    live = (lax.broadcasted_iota(jnp.int32, (1, width), 1) % TOKENS) < live_tokens
    scores = lax.dot_general(key, query, NT, preferred_element_type=jnp.float32)
    prob_grad = lax.dot_general(value, grad, NT, preferred_element_type=jnp.float32)
    scores = jnp.where(allowed, scores, jnp.float32(-1e30))
    peak = jnp.max(scores, axis=0, keepdims=True)
    expo = jnp.exp2((scores - peak) * LOG_SCALE)
    share = jnp.where(live, 1.0 / jnp.sum(expo, axis=0, keepdims=True), 0.0)
    prob = expo * share
    value_grad = jnp.dot(prob.astype(jnp.bfloat16), grad, preferred_element_type=jnp.float32)
    row_total = jnp.sum(prob * prob_grad, axis=0, keepdims=True)
    score_grad = (prob * (prob_grad - row_total) * INV_ROOT).astype(jnp.bfloat16)
    key_grad = jnp.dot(score_grad, query, preferred_element_type=jnp.float32)
    query_grad = lax.dot_general(score_grad, key, TN, preferred_element_type=jnp.float32)
    return (
        (query_grad * factor).astype(jnp.bfloat16),
        (key_grad * factor).astype(jnp.bfloat16),
        (value_grad * factor).astype(jnp.bfloat16),
    )


def kernel(groups, parts, two_ways, *refs):
    facts_ref, kv_ref, q_ref = refs[:3]
    out_q, out_kv, dq, dkv, sem = refs[-5:]
    n_grads = 1 + max(max(p[0], -1 if p[1] is None else p[1]) for p in parts)
    grads = refs[3 : 3 + n_grads]
    turned_ref = refs[3 + n_grads] if two_ways else None
    live_tokens, far, turn, factor = facts_of(facts_ref)
    copies = []
    for at, group in enumerate(groups):
        queries, gradients = [], []
        for head in range(at * GROUP, (at + 1) * GROUP):
            q = q_ref[:, head * HEAD : (head + 1) * HEAD]
            if two_ways:
                q = jnp.where(turn, turned_ref[:, head * HEAD : (head + 1) * HEAD], q)
            queries.append(q)
            plain, other, column, other_column = parts[head]
            g = grads[plain][:, column : column + HEAD]
            if other is not None:
                g = jnp.where(far, grads[other][:, other_column : other_column + HEAD], g)
            gradients.append(g)
        key = kv_ref[:, group * HEAD : (group + 1) * HEAD]
        value = kv_ref[:, (KV_HEADS + group) * HEAD : (KV_HEADS + group + 1) * HEAD]
        query_grad, key_grad, value_grad = one_group(
            live_tokens, factor, jnp.concatenate(queries, 0), key, value, jnp.concatenate(gradients, 0)
        )
        for t in range(GROUP):
            dq[at, :, t * HEAD : (t + 1) * HEAD] = query_grad[t * TOKENS : (t + 1) * TOKENS]
        dkv[2 * at] = key_grad
        dkv[2 * at + 1] = value_grad
        span = GROUP * HEAD
        for n, (src, dst) in enumerate(
            (
                (dq.at[at], out_q.at[:, group * span : (group + 1) * span]),
                (dkv.at[2 * at], out_kv.at[:, group * HEAD : (group + 1) * HEAD]),
                (dkv.at[2 * at + 1], out_kv.at[:, (KV_HEADS + group) * HEAD : (KV_HEADS + group + 1) * HEAD]),
            )
        ):
            copy = pltpu.make_async_copy(src, dst, sem.at[3 * at + n])
            copy.start()
            copies.append(copy)
    for copy in copies:
        copy.wait()


def attend(groups, parts, facts, arrays, outputs=(), two_ways=False):
    vmem = pl.BlockSpec(memory_space=pltpu.VMEM)
    hbm = pl.BlockSpec(memory_space=pl.ANY)
    count = len(groups)
    operands = (facts, *arrays, *outputs)
    first = 1 + len(arrays)
    elements = count * GROUP * TOKENS * HEAD
    return pl.pallas_call(
        functools.partial(kernel, groups, parts, two_ways),
        out_shape=(
            jax.ShapeDtypeStruct((TOKENS, KV_HEADS * GROUP * HEAD), jnp.bfloat16),
            jax.ShapeDtypeStruct((TOKENS, 2 * KV_HEADS * HEAD), jnp.bfloat16),
        ),
        in_specs=[vmem] * first + [hbm] * len(outputs),
        out_specs=(hbm, hbm),
        scratch_shapes=[
            pltpu.VMEM((count, TOKENS, GROUP * HEAD), jnp.bfloat16),
            pltpu.VMEM((2 * count, TOKENS, HEAD), jnp.bfloat16),
            pltpu.SemaphoreType.DMA((3 * count,)),
        ],
        input_output_aliases={first + i: i for i in range(len(outputs))},
        compiler_params=pltpu.CompilerParams(vmem_limit_bytes=24 << 20),
        cost_estimate=pl.CostEstimate(flops=10 * elements * TOKENS, bytes_accessed=6 * elements, transcendentals=elements),
    )(*operands)


def across(column):
    return lambda y, z, x: (y - 1 + z, z + 1, 3) if x == column else None


def body(stash_q, stash_kv, upstream, lengths, domains, domain_weight):
    section = lax.axis_index("section")
    x = section % NX
    span = GROUP * HEAD
    kv = moved(stash_kv, opposite)
    q_most = moved(stash_q[..., : 3 * span], opposite)
    last_part = stash_q[..., 3 * span :]
    q_last = moved_each(last_part, lambda y, z, r: None if turned(y, z, r) else (y + 4, r))
    q_mid = moved_each(last_part, lambda y, z, r: (y + 1, r ^ 2) if turned(y, z, r) else None)
    q_turned = moved_each(q_mid, lambda y, z, r: (y + 3, r ^ 2) if turned(y - 1, z, r) else None)
    part = lambda group: upstream[..., group * span : (group + 1) * span]
    beside = lambda column: lambda y, z, x: (y, z, column) if x == 0 else None
    b_mid = moved(part(1), beside(3))
    c_mid = moved(part(2), beside(1))
    d_mid = moved(part(3), beside(2))
    near = moved(upstream, lambda y, z, x: (y, z, x - 1) if x else None)
    a_far = moved(part(0), across(0))
    b_far = moved(b_mid, across(3))
    c_far = moved(c_mid, across(1))
    d_far = moved(d_mid, across(2))
    y, z, replica = section // (NZ * NX), section // NX % NZ, lax.axis_index("dp")
    flags = jnp.stack([x == NX - 1, turned(y, z, replica)])
    own = jnp.concatenate([lengths, domains, flags]).astype(jnp.float32)
    to = jnp.arange(REPLICAS, dtype=jnp.float32)[:, None]
    row = lambda v: jnp.broadcast_to(v[None], (REPLICAS, v.shape[0]))
    facts = jnp.concatenate([row(own), to, row(domain_weight)], axis=1)
    facts = lax.all_to_all(facts, "dp", 0, 0, tiled=True)
    flat = lambda a: a.reshape(a.shape[2:])
    column = lambda h: (h % GROUP) * HEAD
    parts = [(0, 1 + g, column(h) + g * span, column(h)) for g in range(3) for h in range(GROUP)]
    arrays = (kv, q_most, near, a_far, b_far, c_far)
    outs = attend((0, 1, 2), parts, facts, [flat(a) for a in arrays])
    last = [(0, 1, column(h) + 3 * span, column(h)) for h in range(GROUP)]
    arrays = (kv, q_last, near, d_far, q_turned)
    out_q, out_kv = attend((3,), last, facts, [flat(a) for a in arrays], outs, True)
    return out_q[None, None], out_kv[None, None]


def solution(mesh):
    spec = P("section", "dp", None, None)
    return jax.shard_map(
        body,
        mesh=mesh,
        in_specs=(spec, spec, spec, P("dp"), P("dp"), P()),
        out_specs=(spec, spec),
        check_vma=False,
    )
```

```python
import functools
import math

import jax
import jax.numpy as jnp
from jax import lax
from jax.experimental import pallas as pl
from jax.experimental.pallas import tpu as pltpu
from jax.sharding import PartitionSpec as P

KV_HEADS = 4
GROUP = 8
HEAD = 128
DOMAINS = 7
TOKENS = 128
REPLICAS = 12
NY, NZ, NX = 8, 2, 4

INV_ROOT = 1.0 / math.sqrt(HEAD)
LOG_SCALE = INV_ROOT * math.log2(math.e)
NT = (((1,), (1,)), ((), ()))
TN = (((0,), (0,)), ((), ()))


def section_pairs(move):
    pairs = []
    for y in range(NY):
        for z in range(NZ):
            for x in range(NX):
                to = move(y, z, x)
                if to is not None:
                    ty, tz, tx = to
                    pairs.append(((y * NZ + z) * NX + x, ((ty % NY) * NZ + tz % NZ) * NX + tx % NX))
    return pairs


def device_pairs(move):
    pairs = []
    for y in range(NY):
        for z in range(NZ):
            for x in range(NX):
                for r in range(REPLICAS):
                    to = move(y, z, r)
                    if to is not None:
                        ty, tr = to
                        section = lambda v: ((v % NY) * NZ + z) * NX + x
                        pairs.append((section(y) * REPLICAS + r, section(ty) * REPLICAS + tr))
    return pairs


def moved_each(array, move):
    return lax.ppermute(array, ("section", "dp"), device_pairs(move))


def turned(y, z, replica):
    return (z == 1) & (replica % 2 == 0) & (y % 4 == 1)


def moved(array, move):
    return lax.ppermute(array, "section", section_pairs(move))


def opposite(y, z, x):
    return y + 4, z, x


def facts_of(facts_ref):
    facts = facts_ref[...]
    row = lax.broadcasted_iota(jnp.int32, (REPLICAS, 1), 0).astype(jnp.float32)
    own = jnp.sum(jnp.where(row == facts[:, 4:5], facts, 0.0), axis=0, keepdims=True)
    lengths, domains = facts[:, 0:1], facts[:, 1:2]
    domain = own[:, 1:2]
    total = jnp.sum(lengths, axis=0, keepdims=True)
    count = jnp.sum(jnp.where(domains == domain, lengths, 0.0), axis=0, keepdims=True)
    ids = lax.broadcasted_iota(jnp.int32, (1, DOMAINS), 1).astype(jnp.float32)
    weight = jnp.sum(jnp.where(ids == domain, own[:, 5 : 5 + DOMAINS], 0.0), axis=1, keepdims=True)
    return own[:, 0:1].astype(jnp.int32), own[:, 2:3] > 0.5, own[:, 3:4] > 0.5, weight * total / (DOMAINS * count)


def one_group(live_tokens, factor, query, key, value, grad):
    width = GROUP * TOKENS
    j = lax.broadcasted_iota(jnp.int32, (TOKENS, width), 0)
    i = lax.broadcasted_iota(jnp.int32, (TOKENS, width), 1) % TOKENS
    allowed = (j <= i) & (j < live_tokens)
    live = (lax.broadcasted_iota(jnp.int32, (1, width), 1) % TOKENS) < live_tokens
    scores = lax.dot_general(key, query, NT, preferred_element_type=jnp.float32)
    prob_grad = lax.dot_general(value, grad, NT, preferred_element_type=jnp.float32)
    scores = jnp.where(allowed, scores, jnp.float32(-1e30))
    peak = jnp.max(scores, axis=0, keepdims=True)
    expo = jnp.exp2((scores - peak) * LOG_SCALE)
    share = jnp.where(live, 1.0 / jnp.sum(expo, axis=0, keepdims=True), 0.0)
    prob = expo * share
    value_grad = jnp.dot(prob.astype(jnp.bfloat16), grad, preferred_element_type=jnp.float32)
    row_total = jnp.sum(prob * prob_grad, axis=0, keepdims=True)
    score_grad = (prob * (prob_grad - row_total) * INV_ROOT).astype(jnp.bfloat16)
    key_grad = jnp.dot(score_grad, query, preferred_element_type=jnp.float32)
    query_grad = lax.dot_general(score_grad, key, TN, preferred_element_type=jnp.float32)
    return (
        (query_grad * factor).astype(jnp.bfloat16),
        (key_grad * factor).astype(jnp.bfloat16),
        (value_grad * factor).astype(jnp.bfloat16),
    )


def kernel(groups, parts, two_ways, *refs):
    facts_ref, kv_ref, q_ref = refs[:3]
    out_q, out_kv, dq, dkv, sem = refs[-5:]
    n_grads = 1 + max(max(p[0], -1 if p[1] is None else p[1]) for p in parts)
    grads = refs[3 : 3 + n_grads]
    turned_ref = refs[3 + n_grads] if two_ways else None
    live_tokens, far, turn, factor = facts_of(facts_ref)
    copies = []
    for at, group in enumerate(groups):
        queries, gradients = [], []
        for head in range(at * GROUP, (at + 1) * GROUP):
            q = q_ref[:, head * HEAD : (head + 1) * HEAD]
            if two_ways:
                q = jnp.where(turn, turned_ref[:, head * HEAD : (head + 1) * HEAD], q)
            queries.append(q)
            plain, other, column, other_column = parts[head]
            g = grads[plain][:, column : column + HEAD]
            if other is not None:
                g = jnp.where(far, grads[other][:, other_column : other_column + HEAD], g)
            gradients.append(g)
        key = kv_ref[:, group * HEAD : (group + 1) * HEAD]
        value = kv_ref[:, (KV_HEADS + group) * HEAD : (KV_HEADS + group + 1) * HEAD]
        query_grad, key_grad, value_grad = one_group(
            live_tokens, factor, jnp.concatenate(queries, 0), key, value, jnp.concatenate(gradients, 0)
        )
        for t in range(GROUP):
            dq[at, :, t * HEAD : (t + 1) * HEAD] = query_grad[t * TOKENS : (t + 1) * TOKENS]
        dkv[2 * at] = key_grad
        dkv[2 * at + 1] = value_grad
        span = GROUP * HEAD
        for n, (src, dst) in enumerate(
            (
                (dq.at[at], out_q.at[:, group * span : (group + 1) * span]),
                (dkv.at[2 * at], out_kv.at[:, group * HEAD : (group + 1) * HEAD]),
                (dkv.at[2 * at + 1], out_kv.at[:, (KV_HEADS + group) * HEAD : (KV_HEADS + group + 1) * HEAD]),
            )
        ):
            copy = pltpu.make_async_copy(src, dst, sem.at[3 * at + n])
            copy.start()
            copies.append(copy)
    for copy in copies:
        copy.wait()


def attend(groups, parts, facts, arrays, outputs=(), two_ways=False):
    vmem = pl.BlockSpec(memory_space=pltpu.VMEM)
    hbm = pl.BlockSpec(memory_space=pl.ANY)
    count = len(groups)
    operands = (facts, *arrays, *outputs)
    first = 1 + len(arrays)
    elements = count * GROUP * TOKENS * HEAD
    return pl.pallas_call(
        functools.partial(kernel, groups, parts, two_ways),
        out_shape=(
            jax.ShapeDtypeStruct((TOKENS, KV_HEADS * GROUP * HEAD), jnp.bfloat16),
            jax.ShapeDtypeStruct((TOKENS, 2 * KV_HEADS * HEAD), jnp.bfloat16),
        ),
        in_specs=[vmem] * first + [hbm] * len(outputs),
        out_specs=(hbm, hbm),
        scratch_shapes=[
            pltpu.VMEM((count, TOKENS, GROUP * HEAD), jnp.bfloat16),
            pltpu.VMEM((2 * count, TOKENS, HEAD), jnp.bfloat16),
            pltpu.SemaphoreType.DMA((3 * count,)),
        ],
        input_output_aliases={first + i: i for i in range(len(outputs))},
        compiler_params=pltpu.CompilerParams(vmem_limit_bytes=24 << 20),
        cost_estimate=pl.CostEstimate(flops=10 * elements * TOKENS, bytes_accessed=6 * elements, transcendentals=elements),
    )(*operands)


def cut_kernel(spans, *refs):
    sources, pieces, sem = refs[:2], refs[2:-1], refs[-1]
    copies = []
    for n, (piece, (source, first, last)) in enumerate(zip(pieces, spans)):
        copies.append(pltpu.make_async_copy(sources[source].at[:, first:last], piece, sem.at[n]))
        copies[-1].start()
    for copy in copies:
        copy.wait()


def cut(query, grad):
    span = GROUP * HEAD
    spans = [(0, 0, 3 * span), (0, 3 * span, 4 * span)] + [(1, g * span, (g + 1) * span) for g in range(KV_HEADS)]
    return pl.pallas_call(
        functools.partial(cut_kernel, spans),
        out_shape=[jax.ShapeDtypeStruct((TOKENS, last - first), jnp.bfloat16) for _, first, last in spans],
        in_specs=[pl.BlockSpec(memory_space=pl.ANY)] * 2,
        out_specs=[pl.BlockSpec(memory_space=pltpu.VMEM)] * len(spans),
        scratch_shapes=[pltpu.SemaphoreType.DMA((len(spans),))],
        compiler_params=pltpu.CompilerParams(vmem_limit_bytes=24 << 20),
        cost_estimate=pl.CostEstimate(flops=0, bytes_accessed=4 * TOKENS * 8 * span, transcendentals=0),
        name="cut",
    )(query, grad)


def across(column):
    return lambda y, z, x: (y - 1 + z, z + 1, 3) if x == column else None


def body(stash_q, stash_kv, upstream, lengths, domains, domain_weight):
    section = lax.axis_index("section")
    x = section % NX
    span = GROUP * HEAD
    kv = moved(stash_kv, opposite)
    first_part, last_part, *parts = [a[None, None] for a in cut(stash_q[0, 0], upstream[0, 0])]
    q_most = moved(first_part, opposite)
    q_last = moved_each(last_part, lambda y, z, r: None if turned(y, z, r) else (y + 4, r))
    q_mid = moved_each(last_part, lambda y, z, r: (y + 1, r ^ 2) if turned(y, z, r) else None)
    q_turned = moved_each(q_mid, lambda y, z, r: (y + 3, r ^ 2) if turned(y - 1, z, r) else None)
    part = lambda group: parts[group]
    beside = lambda column: lambda y, z, x: (y, z, column) if x == 0 else None
    b_mid = moved(part(1), beside(3))
    c_mid = moved(part(2), beside(1))
    d_mid = moved(part(3), beside(2))
    near = moved(upstream, lambda y, z, x: (y, z, x - 1) if x else None)
    a_far = moved(part(0), across(0))
    b_far = moved(b_mid, across(3))
    c_far = moved(c_mid, across(1))
    d_far = moved(d_mid, across(2))
    y, z, replica = section // (NZ * NX), section // NX % NZ, lax.axis_index("dp")
    flags = jnp.stack([x == NX - 1, turned(y, z, replica)])
    own = jnp.concatenate([lengths, domains, flags]).astype(jnp.float32)
    to = jnp.arange(REPLICAS, dtype=jnp.float32)[:, None]
    row = lambda v: jnp.broadcast_to(v[None], (REPLICAS, v.shape[0]))
    facts = jnp.concatenate([row(own), to, row(domain_weight)], axis=1)
    facts = lax.all_to_all(facts, "dp", 0, 0, tiled=True)
    flat = lambda a: a.reshape(a.shape[2:])
    column = lambda h: (h % GROUP) * HEAD
    parts = [(0, 1 + g, column(h) + g * span, column(h)) for g in range(3) for h in range(GROUP)]
    arrays = (kv, q_most, near, a_far, b_far, c_far)
    outs = attend((0, 1, 2), parts, facts, [flat(a) for a in arrays])
    last = [(0, 1, column(h) + 3 * span, column(h)) for h in range(GROUP)]
    arrays = (kv, q_last, near, d_far, q_turned)
    out_q, out_kv = attend((3,), last, facts, [flat(a) for a in arrays], outs, True)
    return out_q[None, None], out_kv[None, None]


def solution(mesh):
    spec = P("section", "dp", None, None)
    return jax.shard_map(
        body,
        mesh=mesh,
        in_specs=(spec, spec, spec, P("dp"), P("dp"), P()),
        out_specs=(spec, spec),
        check_vma=False,
    )
```
